32 devices in a mesh: layer: 32 (over z, y, x, core).
Axes of the slice: x: 2, y: 2, z: 4, core: 2. Of those that a mesh axis runs over, the one named last changes fastest.
Arguments:
- lower_block: float32 [32, 512, 512], P('layer'), may hold values from -0.109375 to 0.109375
- upper_block: float32 [32, 512, 512], P('layer'), may hold values from -0.109375 to 0.109375
- right_side: float32 [32, 64, 512], P('layer'), may hold values from -6 to 6
Outputs:
- reduced_lower: float32 [32, 512, 512], P('layer')
- reduced_upper: float32 [32, 512, 512], P('layer')
- reduced_rhs: float32 [32, 64, 512], P('layer')
The draws below stay inside these ranges and needn't reach their ends.
All inputs are finite; a program needn't handle non-finite values.
Results may differ from the reference program's by a relative error of at most 0.00022.
Values sent between devices are 32-bit elements; how exact they have to be, the bound alone decides.
A program may use at most 64 MiB of HBM per device.

```python
import math
import jax
import jax.numpy as jnp
from jax import lax

BLOCK = 512
COLUMNS = 64
LEVELS = 3
CHAINS = 8
LAYERS = 32


def block_scale(key, dims, shards, low, largest):
    level, own = 1.0, jax.random.fold_in(key, 6)
    for axis_at, blocks in shards:
        draws = jnp.exp(jax.random.uniform(jax.random.fold_in(own, axis_at), (blocks,), jnp.float32, low / len(shards), largest / len(shards)))
        level = level * jnp.repeat(draws, dims[axis_at] // blocks).reshape([-1 if axis == axis_at else 1 for axis in range(len(dims))])
    return level


def normal_values(key, dims, deviation, bound, pieces=(), kind=jnp.bfloat16):
    factor_of = block_scale(key, dims, pieces, -0.22, 0.18) if pieces else 1.0
    drawn = jax.random.normal(key, dims, jnp.float32) * deviation * factor_of
    return jnp.minimum(jnp.maximum(drawn, -bound), bound).astype(kind)


def setup_inputs(seed: int = 0) -> dict:
    key_list = jax.random.split(jax.random.key(seed), 4)
    lower_block = normal_values(key_list[0], (LAYERS, BLOCK, BLOCK), (6 * BLOCK) ** -0.5, 0.109375, ((0, 32),), jnp.float32)
    upper_block = normal_values(key_list[1], (LAYERS, BLOCK, BLOCK), (6 * BLOCK) ** -0.5, 0.109375, ((0, 32),), jnp.float32)
    right_side = normal_values(key_list[2], (LAYERS, COLUMNS, BLOCK), 1.0, 6.0, ((0, 32),), jnp.float32)
    return dict(lower_block=lower_block, upper_block=upper_block, right_side=right_side)


def matmul_high(left, right):
    return jnp.dot(left, right, precision=lax.Precision.HIGHEST, preferred_element_type=jnp.float32)

def rows_times(block, columns):
    return lax.dot_general(columns, block, (((1,), (1,)), ((), ())), precision=lax.Precision.HIGHEST, preferred_element_type=jnp.float32)

def reduce_level(group):
    own, from_below, from_above = group
    own_lower = own[:BLOCK]
    own_upper = own[BLOCK:2 * BLOCK]
    own_rhs = own[2 * BLOCK:]
    identity = jnp.eye(BLOCK, dtype=jnp.float32)
    diagonal = identity - matmul_high(own_lower, from_below[BLOCK:2 * BLOCK]) - matmul_high(own_upper, from_above[:BLOCK])
    initial = 2.0 * identity - diagonal
    inverse = matmul_high(initial, 2.0 * identity - matmul_high(diagonal, initial))
    new_lower = -matmul_high(inverse, matmul_high(own_lower, from_below[:BLOCK]))
    new_upper = -matmul_high(inverse, matmul_high(own_upper, from_above[BLOCK:2 * BLOCK]))
    new_rhs = own_rhs - rows_times(own_lower, from_below[2 * BLOCK:]) - rows_times(own_upper, from_above[2 * BLOCK:])
    new_rhs = rows_times(inverse, new_rhs)
    return jnp.concatenate([new_lower, new_upper, new_rhs], axis=0)

def reference(lower_block, upper_block, right_side):
    layers = lower_block.shape[0]
    payload = jnp.concatenate([lower_block, upper_block, right_side], axis=1)
    for level_index in range(LEVELS):
        stride = 2 ** level_index
        from_below = jnp.roll(payload, stride, axis=0)
        from_above = jnp.roll(payload, -stride, axis=0)
        payload = lax.map(reduce_level, (payload, from_below, from_above))
    chain_len = layers // CHAINS
    payload = payload.reshape(chain_len, CHAINS, payload.shape[1], payload.shape[2])
    payload = jnp.transpose(payload, (1, 0, 2, 3)).reshape(layers, payload.shape[2], payload.shape[3])
    factor = 2.5 ** 8 * math.sqrt(BLOCK)
    return (payload[:, :BLOCK] * factor, payload[:, BLOCK:2 * BLOCK] * factor, payload[:, 2 * BLOCK:])
```

```python
import functools
import math

import jax
import jax.numpy as jnp
from jax import lax
from jax.experimental import pallas as pl
from jax.experimental.pallas import tpu as pltpu
from jax.sharding import PartitionSpec as P

LEVELS = 3
CHAINS = 8
F32, BF16 = jnp.float32, jnp.bfloat16
MESH = pl.DeviceIdType.MESH


def halves(value):
    high = value.astype(BF16)
    return high, (value - high.astype(F32)).astype(BF16)


def dot3(a_high, a_low, b_high, b_low, transposed=False):
    dims = (((1,), (1 if transposed else 0,)), ((), ()))
    dot = lambda a, b: lax.dot_general(a, b, dims, preferred_element_type=F32)
    return dot(a_high, b_high) + (dot(a_high, b_low) + dot(a_low, b_high))


def kernel(n, order, columns, factor, lower_ref, upper_ref, rhs_ref, out_lower, out_upper, out_rhs,
           bufs, fin, term, sh, sl, nh, nl, fh, fl, eh, el, qh, ql, yh, yl, xh, xl,
           load_sem, send_sem, recv_sem, fin_send, fin_recv):
    me = lax.axis_index("layer")
    half = order // 2
    chain_len = n // CHAINS
    core = me % 2
    mate = me + 1 - 2 * core
    f = core
    far_step = lambda step, sign: (me + sign * step + n) % n

    def other_core(dev):
        return dev + 1 - 2 * (dev % 2)

    roles = []
    for level in range(2):
        bit = 2 << level
        side = (me // bit) % 2
        across = me + bit * (1 - 2 * side)
        sign = 1 - 2 * side
        roles.append((
            side == core,
            across,
            other_core(across),
            other_core(far_step(2 * bit, sign)),
            other_core(far_step(2 * bit, -sign)),
        ))
    last_far = other_core(far_step(CHAINS, 2 * core - 1))
    chain = 4 * core + 2 * ((me // 4) % 2) + (me // 2) % 2
    goes_to = chain * chain_len + me // CHAINS
    my_chain, my_place = me // chain_len, me % chain_len
    comes_from = CHAINS * my_place + 4 * ((my_chain // 2) % 2) + 2 * (my_chain % 2) + my_chain // 4
    moves = goes_to != me

    def rows_of(piece, first):
        which = (piece // 2 + first) % 2
        return pl.ds(pl.multiple_of(which * order + (piece % 2) * half, half), half)

    def tail_rows():
        return pl.ds(2 * order, columns)

    def remote(level, from_slot, to_slot, flow, piece, rows, dev):
        return pltpu.make_async_remote_copy(
            src_ref=bufs.at[level, from_slot, rows],
            dst_ref=bufs.at[level, to_slot, rows],
            send_sem=send_sem.at[level, flow, piece],
            recv_sem=recv_sem.at[level, to_slot - 1, piece],
            device_id=(dev,),
            device_id_type=MESH,
        )

    def flows(level):
        if level < 2:
            outer, across, diagonal, relay, _ = roles[level]
            return ((outer, 2, 0, across), (jnp.logical_not(outer), 1, 0, diagonal), (jnp.logical_not(outer), 1, 1, mate))
        always = core >= 0
        return ((always, 2, 0, last_far), (always, 1, 1, mate))

    def piece_rows(piece, first):
        return tail_rows() if isinstance(piece, int) and piece == 4 else rows_of(piece, first)

    def send_own(level, piece):
        for when, slot, flow, dev in flows(level):
            @pl.when(when)
            def _():
                remote(level, 0, slot, flow, piece, piece_rows(piece, f), dev).start()

    barrier = pltpu.get_barrier_semaphore()

    def greet(dev):
        pl.semaphore_signal(barrier, inc=1, device_id=(dev,), device_id_type=MESH)

    loads = []
    for index, (ref, start, size) in enumerate(((upper_ref, 0, order), (lower_ref, order, order), (rhs_ref, 2 * order, columns))):
        copy = pltpu.make_async_copy(ref.at[0], bufs.at[0, 0, pl.ds(start, size)], load_sem.at[index])
        copy.start()
        loads.append(copy)

    for level in range(2):
        outer, across, diagonal, relay, relayed_by = roles[level]

        @pl.when(outer)
        def _():
            greet(mate)
            greet(relayed_by)

        @pl.when(jnp.logical_not(outer))
        def _():
            greet(diagonal)
            greet(across)

    greet(mate)
    greet(last_far)

    @pl.when(moves)
    def _():
        greet(comes_from)

    expected = 2 + moves.astype(jnp.int32)
    for level in range(2):
        expected += jnp.where(roles[level][0], 1, 3)
    pl.semaphore_wait(barrier, expected)

    for copy in loads:
        copy.wait()
    for piece in range(5):
        send_own(0, piece)

    def block(r):
        return pl.ds(pl.multiple_of(r * half, half), half)

    def split_into(level, slot, which, high_ref, low_ref):
        @pl.loop(0, 2)
        def _(r):
            rows = pl.ds(pl.multiple_of(which * order + r * half, half), half)
            high, low = halves(bufs[level, slot, rows, :])
            high_ref[which, block(r), :] = high
            low_ref[which, block(r), :] = low

    def multiply(a_high, a_low, b_high, b_low, done):
        @pl.loop(0, 2)
        def _(r):
            done(r, dot3(a_high[block(r), :], a_low[block(r), :], b_high[...], b_low[...]))

    def store_split(high_ref, low_ref):
        def done(r, value):
            high, low = halves(value)
            high_ref[block(r), :] = high
            low_ref[block(r), :] = low
        return done

    for level in range(LEVELS):
        if level < 2:
            outer, across, diagonal, relay, _ = roles[level]
            inner = jnp.logical_not(outer)
            self_slot = jnp.where(outer, 0, 1)
            first = jnp.where(outer, 1 - f, f)
        else:
            outer, inner, relay = core >= 0, None, None
            self_slot = 0
            first = 1 - f
        near_slot = 1 - self_slot

        def wait_slot(slot, piece, rows):
            remote(level, 0, slot, 0, piece, rows, mate).wait_recv()

        def take_far(piece):
            wait_slot(2, piece, piece_rows(piece, first))

        if inner is not None:
            @pl.when(inner)
            def _():
                for piece in range(5):
                    take_far(piece)
                    remote(level, 2, 2, 2, piece, piece_rows(piece, first), relay).start()

        for piece in range(5):
            wait_slot(1, piece, piece_rows(piece, 1 - f))

        for which in range(2):
            split_into(level, self_slot, which, sh, sl)
            split_into(level, near_slot, which, nh, nl)

        def add_term(r, value):
            term[block(r), :] = value

        multiply(sh.at[f], sl.at[f], nh.at[1 - f], nl.at[1 - f], add_term)
        multiply(sh.at[f], sl.at[f], nh.at[f], nl.at[f], store_split(xh.at[f], xl.at[f]))

        @pl.when(outer)
        def _():
            for piece in range(5):
                take_far(piece)

        split_into(level, 2, 0, fh, fl)
        split_into(level, 2, 1, fh, fl)

        def finish_e(r, value):
            high, low = halves(term[block(r), :] + value)
            eh[block(r), :] = high
            el[block(r), :] = low

        multiply(sh.at[1 - f], sl.at[1 - f], fh.at[f], fl.at[f], finish_e)
        multiply(eh, el, eh, el, store_split(qh, ql))

        def finish_y(r, value):
            rows = lax.broadcasted_iota(jnp.int32, (half, order), 0) + r * half
            cols = lax.broadcasted_iota(jnp.int32, (half, order), 1)
            eye = jnp.where(rows == cols, 1.0, 0.0).astype(F32)
            e = eh[block(r), :].astype(F32) + el[block(r), :].astype(F32)
            q = qh[block(r), :].astype(F32) + ql[block(r), :].astype(F32)
            high, low = halves(eye + (e + (q + value)))
            yh[block(r), :] = high
            yl[block(r), :] = low

        multiply(eh, el, qh, ql, finish_y)

        def emit(piece):
            which = (piece // 2 + f) % 2
            r = piece % 2
            value = dot3(yh[block(r), :], yl[block(r), :], xh[which], xl[which])
            rows = rows_of(piece, f)
            if level < LEVELS - 1:
                bufs[level + 1, 0, rows, :] = -value
                send_own(level + 1, piece)
            else:
                fin[rows, :] = value * (-factor)
                send_fin(piece, which, r)

        def fin_copy(piece, out, out_rows, rows):
            return pltpu.make_async_remote_copy(
                src_ref=fin.at[rows], dst_ref=out.at[0, out_rows],
                send_sem=fin_send.at[piece], recv_sem=fin_recv.at[piece],
                device_id=(goes_to,), device_id_type=MESH)

        def fin_local(piece, out, out_rows, rows):
            return pltpu.make_async_copy(fin.at[rows], out.at[0, out_rows], load_sem.at[piece])

        def send_fin_to(out, key, out_rows, rows):
            @pl.when(moves)
            def _():
                fin_copy(key, out, out_rows, rows).start()

            @pl.when(jnp.logical_not(moves))
            def _():
                fin_local(key, out, out_rows, rows).start()

        def send_fin(piece, which, r):
            rows = rows_of(piece, f)

            @pl.when(which == 0)
            def _():
                send_fin_to(out_upper, r, block(r), rows)

            @pl.when(which == 1)
            def _():
                send_fin_to(out_lower, 2 + r, block(r), rows)

        @pl.loop(0, 2)
        def _(piece):
            emit(piece)

        multiply(sh.at[1 - f], sl.at[1 - f], fh.at[1 - f], fl.at[1 - f], store_split(xh.at[1 - f], xl.at[1 - f]))

        @pl.loop(2, 4)
        def _(piece):
            emit(piece)

        near_high, near_low = halves(bufs[level, near_slot, tail_rows(), :])
        far_high, far_low = halves(bufs[level, 2, tail_rows(), :])
        right = (bufs[level, self_slot, tail_rows(), :]
                 - dot3(near_high, near_low, sh[f], sl[f], True)
                 - dot3(far_high, far_low, sh[1 - f], sl[1 - f], True))
        right_high, right_low = halves(right)
        right = dot3(right_high, right_low, yh[...], yl[...], True)
        if level < LEVELS - 1:
            bufs[level + 1, 0, tail_rows(), :] = right
            send_own(level + 1, 4)
        else:
            fin[tail_rows(), :] = right
            send_fin_to(out_rhs, 4, pl.ds(0, columns), tail_rows())

    for level in range(LEVELS):
        for when, slot, flow, dev in flows(level):
            @pl.when(when)
            def _():
                for piece in range(5):
                    remote(level, 0, slot, flow, piece, piece_rows(piece, f), dev).wait_send()
        if level < 2:
            outer, across, diagonal, relay, _ = roles[level]

            @pl.when(jnp.logical_not(outer))
            def _():
                for piece in range(5):
                    remote(level, 2, 2, 2, piece, piece_rows(piece, f), relay).wait_send()

    ends = [(r + 2 * w, out, pl.ds(r * half, half), pl.ds(w * order + r * half, half))
            for w, out in ((0, out_upper), (1, out_lower)) for r in range(2)]
    ends.append((4, out_rhs, pl.ds(0, columns), tail_rows()))
    for key, out, out_rows, rows in ends:
        @pl.when(moves)
        def _():
            copy = fin_copy(key, out, out_rows, rows)
            copy.wait_send()
            copy.wait_recv()

        @pl.when(jnp.logical_not(moves))
        def _():
            fin_local(key, out, out_rows, rows).wait()


def per_device(lower_block, upper_block, right_side):
    n = lax.axis_size("layer")
    order, columns = lower_block.shape[2], right_side.shape[1]
    rows = 2 * order + columns
    pair = lambda: pltpu.VMEM((2, order, order), BF16)
    one = lambda: pltpu.VMEM((order, order), BF16)
    return pl.pallas_call(
        functools.partial(kernel, n, order, columns, 2.5**8 * math.sqrt(order)),
        out_shape=[jax.ShapeDtypeStruct(a.shape, F32) for a in (lower_block, upper_block, right_side)],
        in_specs=[pl.BlockSpec(memory_space=pl.ANY)] * 3,
        out_specs=[pl.BlockSpec(memory_space=pltpu.VMEM)] * 3,
        scratch_shapes=[
            pltpu.VMEM((LEVELS, 3, rows, order), F32),
            pltpu.VMEM((rows, order), F32),
            pltpu.VMEM((order, order), F32),
            pair(), pair(), pair(), pair(), pair(), pair(),
            one(), one(), one(), one(), one(), one(),
            pair(), pair(),
            pltpu.SemaphoreType.DMA((5,)),
            pltpu.SemaphoreType.DMA((LEVELS, 3, 5)),
            pltpu.SemaphoreType.DMA((LEVELS, 2, 5)),
            pltpu.SemaphoreType.DMA((5,)),
            pltpu.SemaphoreType.DMA((5,)),
        ],
        compiler_params=pltpu.CompilerParams(
            collective_id=0, has_side_effects=True, vmem_limit_bytes=60 * 1024 * 1024
        ),
    )(lower_block, upper_block, right_side)


def solution(mesh):
    placed = (P("layer", None, None), P("layer", None, None), P("layer", None, None))
    return jax.shard_map(
        per_device,
        mesh=mesh,
        in_specs=placed,
        out_specs=placed,
        check_vma=False,
    )
```

```python
import functools
import math

import jax
import jax.numpy as jnp
from jax import lax
from jax.experimental import pallas as pl
from jax.experimental.pallas import tpu as pltpu
from jax.sharding import PartitionSpec as P

LEVELS = 3
CHAINS = 8
F32, BF16 = jnp.float32, jnp.bfloat16
MESH = pl.DeviceIdType.MESH


def halves(value):
    high = value.astype(BF16)
    return high, (value - high.astype(F32)).astype(BF16)


def dot3(a_high, a_low, b_high, b_low, transposed=False):
    dims = (((1,), (1 if transposed else 0,)), ((), ()))
    dot = lambda a, b: lax.dot_general(a, b, dims, preferred_element_type=F32)
    return dot(a_high, b_high) + (dot(a_high, b_low) + dot(a_low, b_high))


def kernel(n, order, columns, factor, lower_ref, upper_ref, rhs_ref, out_lower, out_upper, out_rhs,
           bufs, fin, term, sh, sl, nh, nl, fh, fl, eh, el, qh, ql, yh, yl, xh, xl,
           load_sem, send_sem, recv_sem, fin_send, fin_recv, passing, pass_send, pass_recv):
    me = lax.axis_index("layer")
    half = order // 2
    chain_len = n // CHAINS
    core = me % 2
    mate = me + 1 - 2 * core
    f = core
    far_step = lambda step, sign: (me + sign * step + n) % n

    def other_core(dev):
        return dev + 1 - 2 * (dev % 2)

    roles = []
    for level in range(2):
        bit = 2 << level
        side = (me // bit) % 2
        across = me + bit * (1 - 2 * side)
        sign = 1 - 2 * side
        roles.append((
            side == core,
            across,
            other_core(across),
            other_core(far_step(2 * bit, sign)),
            other_core(far_step(2 * bit, -sign)),
        ))
    last_far = other_core(far_step(CHAINS, 2 * core - 1))
    chain = 4 * core + 2 * ((me // 4) % 2) + (me // 2) % 2
    goes_to = chain * chain_len + me // CHAINS
    my_chain, my_place = me // chain_len, me % chain_len
    comes_from = CHAINS * my_place + 4 * ((my_chain // 2) % 2) + 2 * (my_chain % 2) + my_chain // 4
    moves = goes_to != me
    groups = n // CHAINS

    def detour(dev):
        group, side, at_core = dev // CHAINS, (dev // 4) % 2, dev % 2
        low = (group == 1) & (side == 0) & (at_core == 0)
        high = (group == groups - 2) & (side == 1) & (at_core == 1)
        return low | high

    def y_partner(dev):
        return dev + 4 * (1 - 2 * ((dev // 4) % 2))

    def home(dev):
        return (4 * (dev % 2) + 2 * ((dev // 4) % 2) + (dev // 2) % 2) * chain_len + dev // CHAINS

    helped = y_partner(me)
    helps = detour(helped)
    detours = detour(me)
    helped_home = home(helped)
    greets = jnp.where(detour(comes_from), y_partner(comes_from), comes_from)

    def rows_of(piece, first):
        which = (piece // 2 + first) % 2
        return pl.ds(pl.multiple_of(which * order + (piece % 2) * half, half), half)

    def tail_rows():
        return pl.ds(2 * order, columns)

    def remote(level, from_slot, to_slot, flow, piece, rows, dev):
        return pltpu.make_async_remote_copy(
            src_ref=bufs.at[level, from_slot, rows],
            dst_ref=bufs.at[level, to_slot, rows],
            send_sem=send_sem.at[level, flow, piece],
            recv_sem=recv_sem.at[level, to_slot - 1, piece],
            device_id=(dev,),
            device_id_type=MESH,
        )

    def flows(level):
        if level < 2:
            outer, across, diagonal, relay, _ = roles[level]
            return ((outer, 2, 0, across), (jnp.logical_not(outer), 1, 0, diagonal), (jnp.logical_not(outer), 1, 1, mate))
        always = core >= 0
        return ((always, 2, 0, last_far), (always, 1, 1, mate))

    def piece_rows(piece, first):
        return tail_rows() if isinstance(piece, int) and piece == 4 else rows_of(piece, first)

    def send_own(level, piece):
        for at, (when, slot, flow, dev) in enumerate(flows(level)):
            if level < 2 and at == 1:
                continue

            @pl.when(when)
            def _():
                remote(level, 0, slot, flow, piece, piece_rows(piece, f), dev).start()

    def send_held(level, piece):
        _, slot, flow, dev = flows(level)[1]
        remote(level, 0, slot, flow, piece, piece_rows(piece, f), dev).start()

    barrier = pltpu.get_barrier_semaphore()

    def greet(dev):
        pl.semaphore_signal(barrier, inc=1, device_id=(dev,), device_id_type=MESH)

    loads = []
    for index, (ref, start, size) in enumerate(((upper_ref, 0, order), (lower_ref, order, order), (rhs_ref, 2 * order, columns))):
        copy = pltpu.make_async_copy(ref.at[0], bufs.at[0, 0, pl.ds(start, size)], load_sem.at[index])
        copy.start()
        loads.append(copy)

    for level in range(2):
        outer, across, diagonal, relay, relayed_by = roles[level]

        @pl.when(outer)
        def _():
            greet(mate)
            greet(relayed_by)

        @pl.when(jnp.logical_not(outer))
        def _():
            greet(diagonal)
            greet(across)

    greet(mate)
    greet(last_far)

    @pl.when(moves)
    def _():
        greet(greets)

    @pl.when(helps)
    def _():
        greet(helped)

    expected = 2 + moves.astype(jnp.int32) + helps.astype(jnp.int32)
    for level in range(2):
        expected += jnp.where(roles[level][0], 1, 3)
    pl.semaphore_wait(barrier, expected)

    for copy in loads:
        copy.wait()
    for piece in range(5):
        send_own(0, piece)

    def block(r):
        return pl.ds(pl.multiple_of(r * half, half), half)

    def split_into(level, slot, which, high_ref, low_ref):
        @pl.loop(0, 2)
        def _(r):
            rows = pl.ds(pl.multiple_of(which * order + r * half, half), half)
            high, low = halves(bufs[level, slot, rows, :])
            high_ref[which, block(r), :] = high
            low_ref[which, block(r), :] = low

    def multiply(a_high, a_low, b_high, b_low, done):
        @pl.loop(0, 2)
        def _(r):
            done(r, dot3(a_high[block(r), :], a_low[block(r), :], b_high[...], b_low[...]))

    def store_split(high_ref, low_ref):
        def done(r, value):
            high, low = halves(value)
            high_ref[block(r), :] = high
            low_ref[block(r), :] = low
        return done

    def fin_copy(key, out, out_rows, rows):
        return pltpu.make_async_remote_copy(
            src_ref=fin.at[rows], dst_ref=out.at[0, out_rows],
            send_sem=fin_send.at[key], recv_sem=fin_recv.at[key],
            device_id=(goes_to,), device_id_type=MESH)

    def detour_copy(key, rows):
        return pltpu.make_async_remote_copy(
            src_ref=fin.at[rows], dst_ref=passing.at[rows],
            send_sem=fin_send.at[key], recv_sem=pass_recv.at[key],
            device_id=(helped,), device_id_type=MESH)

    def pass_copy(key, out, out_rows, rows):
        return pltpu.make_async_remote_copy(
            src_ref=passing.at[rows], dst_ref=out.at[0, out_rows],
            send_sem=pass_send.at[key], recv_sem=fin_recv.at[key],
            device_id=(helped_home,), device_id_type=MESH)

    def fin_local(key, out, out_rows, rows):
        return pltpu.make_async_copy(fin.at[rows], out.at[0, out_rows], load_sem.at[key])

    def send_fin_to(out, key, out_rows, rows):
        @pl.when(moves & jnp.logical_not(detours))
        def _():
            fin_copy(key, out, out_rows, rows).start()

        @pl.when(detours)
        def _():
            detour_copy(key, rows).start()

        @pl.when(jnp.logical_not(moves))
        def _():
            fin_local(key, out, out_rows, rows).start()

    for level in range(LEVELS):
        if level < 2:
            outer, across, diagonal, relay, _ = roles[level]
            inner = jnp.logical_not(outer)
            self_slot = jnp.where(outer, 0, 1)
            first = jnp.where(outer, 1 - f, f)
        else:
            outer, inner, relay = core >= 0, None, None
            self_slot = 0
            first = 1 - f
        near_slot = 1 - self_slot

        def wait_slot(slot, piece, rows):
            remote(level, 0, slot, 0, piece, rows, mate).wait_recv()

        def take_far(piece):
            wait_slot(2, piece, piece_rows(piece, first))

        if inner is not None:
            @pl.when(inner)
            def _():
                for piece in range(5):
                    take_far(piece)
                    remote(level, 2, 2, 2, piece, piece_rows(piece, first), relay).start()
                    if piece >= 1:
                        send_held(level, piece - 1)
                send_held(level, 4)

        for piece in range(5):
            wait_slot(1, piece, piece_rows(piece, 1 - f))

        for which in range(2):
            split_into(level, self_slot, which, sh, sl)
            split_into(level, near_slot, which, nh, nl)

        def add_term(r, value):
            term[block(r), :] = value

        multiply(sh.at[f], sl.at[f], nh.at[1 - f], nl.at[1 - f], add_term)
        multiply(sh.at[f], sl.at[f], nh.at[f], nl.at[f], store_split(xh.at[f], xl.at[f]))

        @pl.when(outer)
        def _():
            for piece in range(5):
                take_far(piece)

        split_into(level, 2, 0, fh, fl)
        split_into(level, 2, 1, fh, fl)

        def finish_e(r, value):
            high, low = halves(term[block(r), :] + value)
            eh[block(r), :] = high
            el[block(r), :] = low

        multiply(sh.at[1 - f], sl.at[1 - f], fh.at[f], fl.at[f], finish_e)
        multiply(eh, el, eh, el, store_split(qh, ql))

        def finish_y(r, value):
            rows = lax.broadcasted_iota(jnp.int32, (half, order), 0) + r * half
            cols = lax.broadcasted_iota(jnp.int32, (half, order), 1)
            eye = jnp.where(rows == cols, 1.0, 0.0).astype(F32)
            e = eh[block(r), :].astype(F32) + el[block(r), :].astype(F32)
            q = qh[block(r), :].astype(F32) + ql[block(r), :].astype(F32)
            high, low = halves(eye + (e + (q + value)))
            yh[block(r), :] = high
            yl[block(r), :] = low

        multiply(eh, el, qh, ql, finish_y)

        def emit(piece):
            which = (piece // 2 + f) % 2
            r = piece % 2
            value = dot3(yh[block(r), :], yl[block(r), :], xh[which], xl[which])
            rows = rows_of(piece, f)
            if level < LEVELS - 1:
                bufs[level + 1, 0, rows, :] = -value
                send_own(level + 1, piece)
            else:
                fin[rows, :] = value * (-factor)
                send_fin(piece, which, r)

        def send_fin(piece, which, r):
            rows = rows_of(piece, f)

            @pl.when(which == 0)
            def _():
                send_fin_to(out_upper, r, block(r), rows)

            @pl.when(which == 1)
            def _():
                send_fin_to(out_lower, 2 + r, block(r), rows)

        @pl.loop(0, 2)
        def _(piece):
            emit(piece)

        multiply(sh.at[1 - f], sl.at[1 - f], fh.at[1 - f], fl.at[1 - f], store_split(xh.at[1 - f], xl.at[1 - f]))

        @pl.loop(2, 4)
        def _(piece):
            emit(piece)

        near_high, near_low = halves(bufs[level, near_slot, tail_rows(), :])
        far_high, far_low = halves(bufs[level, 2, tail_rows(), :])
        right = (bufs[level, self_slot, tail_rows(), :]
                 - dot3(near_high, near_low, sh[f], sl[f], True)
                 - dot3(far_high, far_low, sh[1 - f], sl[1 - f], True))
        right_high, right_low = halves(right)
        right = dot3(right_high, right_low, yh[...], yl[...], True)
        if level < LEVELS - 1:
            bufs[level + 1, 0, tail_rows(), :] = right
            send_own(level + 1, 4)
        else:
            fin[tail_rows(), :] = right
            send_fin_to(out_rhs, 4, pl.ds(0, columns), tail_rows())

    ends = [(r + 2 * w, out, pl.ds(r * half, half), pl.ds(w * order + r * half, half))
            for w, out in ((0, out_upper), (1, out_lower)) for r in range(2)]
    ends.append((4, out_rhs, pl.ds(0, columns), tail_rows()))

    for at_core, turn in ((0, 0), (1, 2)):
        @pl.when(helps & (core == at_core))
        def _():
            for key, out, out_rows, rows in ends[turn:4] + ends[:turn] + ends[4:]:
                detour_copy(key, rows).wait_recv()
                pass_copy(key, out, out_rows, rows).start()

    for level in range(LEVELS):
        for when, slot, flow, dev in flows(level):
            @pl.when(when)
            def _():
                for piece in range(5):
                    remote(level, 0, slot, flow, piece, piece_rows(piece, f), dev).wait_send()
        if level < 2:
            outer, across, diagonal, relay, _ = roles[level]

            @pl.when(jnp.logical_not(outer))
            def _():
                for piece in range(5):
                    remote(level, 2, 2, 2, piece, piece_rows(piece, f), relay).wait_send()

    for key, out, out_rows, rows in ends:
        @pl.when(moves)
        def _():
            copy = fin_copy(key, out, out_rows, rows)
            copy.wait_send()
            copy.wait_recv()

        @pl.when(helps)
        def _():
            pass_copy(key, out, out_rows, rows).wait_send()

        @pl.when(jnp.logical_not(moves))
        def _():
            fin_local(key, out, out_rows, rows).wait()


def per_device(lower_block, upper_block, right_side):
    n = lax.axis_size("layer")
    order, columns = lower_block.shape[2], right_side.shape[1]
    rows = 2 * order + columns
    pair = lambda: pltpu.VMEM((2, order, order), BF16)
    one = lambda: pltpu.VMEM((order, order), BF16)
    return pl.pallas_call(
        functools.partial(kernel, n, order, columns, 2.5**8 * math.sqrt(order)),
        out_shape=[jax.ShapeDtypeStruct(a.shape, F32) for a in (lower_block, upper_block, right_side)],
        in_specs=[pl.BlockSpec(memory_space=pl.ANY)] * 3,
        out_specs=[pl.BlockSpec(memory_space=pltpu.VMEM)] * 3,
        scratch_shapes=[
            pltpu.VMEM((LEVELS, 3, rows, order), F32),
            pltpu.VMEM((rows, order), F32),
            pltpu.VMEM((order, order), F32),
            pair(), pair(), pair(), pair(), pair(), pair(),
            one(), one(), one(), one(), one(), one(),
            pair(), pair(),
            pltpu.SemaphoreType.DMA((5,)),
            pltpu.SemaphoreType.DMA((LEVELS, 3, 5)),
            pltpu.SemaphoreType.DMA((LEVELS, 2, 5)),
            pltpu.SemaphoreType.DMA((5,)),
            pltpu.SemaphoreType.DMA((5,)),
            pltpu.VMEM((rows, order), F32),
            pltpu.SemaphoreType.DMA((5,)),
            pltpu.SemaphoreType.DMA((5,)),
        ],
        compiler_params=pltpu.CompilerParams(
            collective_id=0, has_side_effects=True, vmem_limit_bytes=60 * 1024 * 1024
        ),
    )(lower_block, upper_block, right_side)


def solution(mesh):
    placed = (P("layer", None, None), P("layer", None, None), P("layer", None, None))
    return jax.shard_map(
        per_device,
        mesh=mesh,
        in_specs=placed,
        out_specs=placed,
        check_vma=False,
    )
```

```python
import functools
import math

import jax
import jax.numpy as jnp
from jax import lax
from jax.experimental import pallas as pl
from jax.experimental.pallas import tpu as pltpu
from jax.sharding import PartitionSpec as P

LEVELS = 3
CHAINS = 8
F32, BF16 = jnp.float32, jnp.bfloat16
MESH = pl.DeviceIdType.MESH


def halves(value):
    high = value.astype(BF16)
    return high, (value - high.astype(F32)).astype(BF16)


def dot3(a_high, a_low, b_high, b_low, transposed=False):
    dims = (((1,), (1 if transposed else 0,)), ((), ()))
    dot = lambda a, b: lax.dot_general(a, b, dims, preferred_element_type=F32)
    return dot(a_high, b_high) + (dot(a_high, b_low) + dot(a_low, b_high))


def kernel(n, order, columns, factor, lower_ref, upper_ref, rhs_ref, out_lower, out_upper, out_rhs,
           bufs, fin, term, sh, sl, nh, nl, fh, fl, eh, el, qh, ql, yh, yl, xh, xl,
           load_sem, send_sem, recv_sem, fin_send, fin_recv, passing, pass_send, pass_recv):
    me = lax.axis_index("layer")
    half = order // 2
    chain_len = n // CHAINS
    core = me % 2
    mate = me + 1 - 2 * core
    f = core
    far_step = lambda step, sign: (me + sign * step + n) % n

    def other_core(dev):
        return dev + 1 - 2 * (dev % 2)

    roles = []
    for level in range(2):
        bit = 2 << level
        side = (me // bit) % 2
        across = me + bit * (1 - 2 * side)
        sign = 1 - 2 * side
        roles.append((
            side == core,
            across,
            other_core(across),
            other_core(far_step(2 * bit, sign)),
            other_core(far_step(2 * bit, -sign)),
        ))
    last_far = other_core(far_step(CHAINS, 2 * core - 1))
    chain = 4 * core + 2 * ((me // 4) % 2) + (me // 2) % 2
    goes_to = chain * chain_len + me // CHAINS
    my_chain, my_place = me // chain_len, me % chain_len
    comes_from = CHAINS * my_place + 4 * ((my_chain // 2) % 2) + 2 * (my_chain % 2) + my_chain // 4
    moves = goes_to != me
    groups = n // CHAINS

    def detour(dev):
        group, side, at_core = dev // CHAINS, (dev // 4) % 2, dev % 2
        low = (group == 1) & (side == 0) & (at_core == 0)
        high = (group == groups - 2) & (side == 1) & (at_core == 1)
        return low | high

    def y_partner(dev):
        return dev + 4 * (1 - 2 * ((dev // 4) % 2))

    def home(dev):
        return (4 * (dev % 2) + 2 * ((dev // 4) % 2) + (dev // 2) % 2) * chain_len + dev // CHAINS

    helped = y_partner(me)
    helps = detour(helped)
    detours = detour(me)
    helped_home = home(helped)
    greets = jnp.where(detour(comes_from), y_partner(comes_from), comes_from)

    def rows_of(piece, first):
        which = (piece // 2 + first) % 2
        return pl.ds(pl.multiple_of(which * order + (piece % 2) * half, half), half)

    def tail_rows():
        return pl.ds(2 * order, columns)

    def remote(level, from_slot, to_slot, flow, piece, rows, dev):
        return pltpu.make_async_remote_copy(
            src_ref=bufs.at[level, from_slot, rows],
            dst_ref=bufs.at[level, to_slot, rows],
            send_sem=send_sem.at[level, flow, piece],
            recv_sem=recv_sem.at[level, to_slot - 1, piece],
            device_id=(dev,),
            device_id_type=MESH,
        )

    def flows(level):
        if level < 2:
            outer, across, diagonal, relay, _ = roles[level]
            return ((outer, 2, 0, across), (jnp.logical_not(outer), 1, 0, diagonal), (jnp.logical_not(outer), 1, 1, mate))
        always = core >= 0
        return ((always, 2, 0, last_far), (always, 1, 1, mate))

    def piece_rows(piece, first):
        return tail_rows() if isinstance(piece, int) and piece == 4 else rows_of(piece, first)

    def send_own(level, piece):
        for at, (when, slot, flow, dev) in enumerate(flows(level)):
            if level < 2 and at == 1:
                continue

            @pl.when(when)
            def _():
                remote(level, 0, slot, flow, piece, piece_rows(piece, f), dev).start()

    def send_held(level, piece):
        _, slot, flow, dev = flows(level)[1]
        remote(level, 0, slot, flow, piece, piece_rows(piece, f), dev).start()

    barrier = pltpu.get_barrier_semaphore()

    def greet(dev):
        pl.semaphore_signal(barrier, inc=1, device_id=(dev,), device_id_type=MESH)

    loads = []
    for index, (ref, start, size) in enumerate(((upper_ref, 0, order), (lower_ref, order, order), (rhs_ref, 2 * order, columns))):
        copy = pltpu.make_async_copy(ref.at[0], bufs.at[0, 0, pl.ds(start, size)], load_sem.at[index])
        copy.start()
        loads.append(copy)

    for level in range(2):
        outer, across, diagonal, relay, relayed_by = roles[level]

        @pl.when(outer)
        def _():
            greet(mate)
            greet(relayed_by)

        @pl.when(jnp.logical_not(outer))
        def _():
            greet(diagonal)
            greet(across)

    greet(mate)
    greet(last_far)

    @pl.when(moves)
    def _():
        greet(greets)

    @pl.when(helps)
    def _():
        greet(helped)

    expected = 2 + moves.astype(jnp.int32) + helps.astype(jnp.int32)
    for level in range(2):
        expected += jnp.where(roles[level][0], 1, 3)
    pl.semaphore_wait(barrier, expected)

    for copy in loads:
        copy.wait()
    for piece in range(5):
        send_own(0, piece)

    def block(r):
        return pl.ds(pl.multiple_of(r * half, half), half)

    def split_into(level, slot, which, high_ref, low_ref):
        @pl.loop(0, 2)
        def _(r):
            rows = pl.ds(pl.multiple_of(which * order + r * half, half), half)
            high, low = halves(bufs[level, slot, rows, :])
            high_ref[which, block(r), :] = high
            low_ref[which, block(r), :] = low

    def multiply(a_high, a_low, b_high, b_low, done):
        @pl.loop(0, 2)
        def _(r):
            done(r, dot3(a_high[block(r), :], a_low[block(r), :], b_high[...], b_low[...]))

    def store_split(high_ref, low_ref):
        def done(r, value):
            high, low = halves(value)
            high_ref[block(r), :] = high
            low_ref[block(r), :] = low
        return done

    def fin_copy(key, out, out_rows, rows):
        return pltpu.make_async_remote_copy(
            src_ref=fin.at[rows], dst_ref=out.at[0, out_rows],
            send_sem=fin_send.at[key], recv_sem=fin_recv.at[key],
            device_id=(goes_to,), device_id_type=MESH)

    def detour_copy(key, rows):
        return pltpu.make_async_remote_copy(
            src_ref=fin.at[rows], dst_ref=passing.at[rows],
            send_sem=fin_send.at[key], recv_sem=pass_recv.at[key],
            device_id=(helped,), device_id_type=MESH)

    def pass_copy(key, out, out_rows, rows):
        return pltpu.make_async_remote_copy(
            src_ref=passing.at[rows], dst_ref=out.at[0, out_rows],
            send_sem=pass_send.at[key], recv_sem=fin_recv.at[key],
            device_id=(helped_home,), device_id_type=MESH)

    def fin_local(key, out, out_rows, rows):
        return pltpu.make_async_copy(fin.at[rows], out.at[0, out_rows], load_sem.at[key])

    def send_fin_to(out, key, out_rows, rows):
        @pl.when(moves & jnp.logical_not(detours))
        def _():
            fin_copy(key, out, out_rows, rows).start()

        @pl.when(detours)
        def _():
            detour_copy(key, rows).start()

        @pl.when(jnp.logical_not(moves))
        def _():
            fin_local(key, out, out_rows, rows).start()

    for level in range(LEVELS):
        if level < 2:
            outer, across, diagonal, relay, _ = roles[level]
            inner = jnp.logical_not(outer)
            self_slot = jnp.where(outer, 0, 1)
            first = jnp.where(outer, 1 - f, f)
        else:
            outer, inner, relay = core >= 0, None, None
            self_slot = 0
            first = 1 - f
        near_slot = 1 - self_slot

        def wait_slot(slot, piece, rows):
            remote(level, 0, slot, 0, piece, rows, mate).wait_recv()

        def take_far(piece):
            wait_slot(2, piece, piece_rows(piece, first))

        if inner is not None:
            @pl.when(inner)
            def _():
                for piece in range(5):
                    take_far(piece)
                    remote(level, 2, 2, 2, piece, piece_rows(piece, first), relay).start()
                    if piece >= 1:
                        send_held(level, piece - 1)
                send_held(level, 4)

        def take_one(piece):
            wait_slot(1, piece, piece_rows(piece, 1 - f))

        def staged(outer_pieces, inner_pieces):
            @pl.when(outer)
            def _():
                for take, piece in outer_pieces:
                    take(piece)

            if inner is not None:
                @pl.when(inner)
                def _():
                    for take, piece in inner_pieces:
                        take(piece)

        early = jnp.where(outer, f, 1 - f)
        late = 1 - early
        one_slot = jnp.where(outer, near_slot, 2)
        two_slot = jnp.where(outer, 2, near_slot)

        staged([(take_one, p) for p in range(5)], [(take_one, 0), (take_one, 1)])
        split_into(level, self_slot, early, sh, sl)
        split_into(level, one_slot, 0, nh, nl)
        split_into(level, one_slot, 1, nh, nl)

        def add_term(r, value):
            term[block(r), :] = value

        multiply(sh.at[early], sl.at[early], nh.at[late], nl.at[late], add_term)
        multiply(sh.at[early], sl.at[early], nh.at[early], nl.at[early], store_split(xh.at[early], xl.at[early]))

        staged([(take_far, 0), (take_far, 1)], [(take_one, 2), (take_one, 3)])
        split_into(level, self_slot, late, sh, sl)
        split_into(level, two_slot, late, fh, fl)
        multiply(sh.at[late], sl.at[late], fh.at[late], fl.at[late], store_split(xh.at[late], xl.at[late]))
        staged([(take_far, 2), (take_far, 3)], [])
        split_into(level, two_slot, early, fh, fl)

        def finish_e(r, value):
            high, low = halves(term[block(r), :] + value)
            eh[block(r), :] = high
            el[block(r), :] = low

        multiply(sh.at[late], sl.at[late], fh.at[early], fl.at[early], finish_e)
        multiply(eh, el, eh, el, store_split(qh, ql))

        def finish_y(r, value):
            rows = lax.broadcasted_iota(jnp.int32, (half, order), 0) + r * half
            cols = lax.broadcasted_iota(jnp.int32, (half, order), 1)
            eye = jnp.where(rows == cols, 1.0, 0.0).astype(F32)
            e = eh[block(r), :].astype(F32) + el[block(r), :].astype(F32)
            q = qh[block(r), :].astype(F32) + ql[block(r), :].astype(F32)
            high, low = halves(eye + (e + (q + value)))
            yh[block(r), :] = high
            yl[block(r), :] = low

        multiply(eh, el, qh, ql, finish_y)

        def emit(piece):
            which = (piece // 2 + f) % 2
            r = piece % 2
            value = dot3(yh[block(r), :], yl[block(r), :], xh[which], xl[which])
            rows = rows_of(piece, f)
            if level < LEVELS - 1:
                bufs[level + 1, 0, rows, :] = -value
                send_own(level + 1, piece)
            else:
                fin[rows, :] = value * (-factor)
                send_fin(piece, which, r)

        def send_fin(piece, which, r):
            rows = rows_of(piece, f)

            @pl.when(which == 0)
            def _():
                send_fin_to(out_upper, r, block(r), rows)

            @pl.when(which == 1)
            def _():
                send_fin_to(out_lower, 2 + r, block(r), rows)

        @pl.loop(0, 4)
        def _(piece):
            emit(piece)

        staged([(take_far, 4)], [(take_one, 4)])
        near_high, near_low = halves(bufs[level, one_slot, tail_rows(), :])
        far_high, far_low = halves(bufs[level, two_slot, tail_rows(), :])
        right = (bufs[level, self_slot, tail_rows(), :]
                 - dot3(near_high, near_low, sh[early], sl[early], True)
                 - dot3(far_high, far_low, sh[late], sl[late], True))
        right_high, right_low = halves(right)
        right = dot3(right_high, right_low, yh[...], yl[...], True)
        if level < LEVELS - 1:
            bufs[level + 1, 0, tail_rows(), :] = right
            send_own(level + 1, 4)
        else:
            fin[tail_rows(), :] = right
            send_fin_to(out_rhs, 4, pl.ds(0, columns), tail_rows())

    ends = [(r + 2 * w, out, pl.ds(r * half, half), pl.ds(w * order + r * half, half))
            for w, out in ((0, out_upper), (1, out_lower)) for r in range(2)]
    ends.append((4, out_rhs, pl.ds(0, columns), tail_rows()))

    for at_core, turn in ((0, 0), (1, 2)):
        @pl.when(helps & (core == at_core))
        def _():
            for key, out, out_rows, rows in ends[turn:4] + ends[:turn] + ends[4:]:
                detour_copy(key, rows).wait_recv()
                pass_copy(key, out, out_rows, rows).start()

    for level in range(LEVELS):
        for when, slot, flow, dev in flows(level):
            @pl.when(when)
            def _():
                for piece in range(5):
                    remote(level, 0, slot, flow, piece, piece_rows(piece, f), dev).wait_send()
        if level < 2:
            outer, across, diagonal, relay, _ = roles[level]

            @pl.when(jnp.logical_not(outer))
            def _():
                for piece in range(5):
                    remote(level, 2, 2, 2, piece, piece_rows(piece, f), relay).wait_send()

    for key, out, out_rows, rows in ends:
        @pl.when(moves)
        def _():
            copy = fin_copy(key, out, out_rows, rows)
            copy.wait_send()
            copy.wait_recv()

        @pl.when(helps)
        def _():
            pass_copy(key, out, out_rows, rows).wait_send()

        @pl.when(jnp.logical_not(moves))
        def _():
            fin_local(key, out, out_rows, rows).wait()


def per_device(lower_block, upper_block, right_side):
    n = lax.axis_size("layer")
    order, columns = lower_block.shape[2], right_side.shape[1]
    rows = 2 * order + columns
    pair = lambda: pltpu.VMEM((2, order, order), BF16)
    one = lambda: pltpu.VMEM((order, order), BF16)
    return pl.pallas_call(
        functools.partial(kernel, n, order, columns, 2.5**8 * math.sqrt(order)),
        out_shape=[jax.ShapeDtypeStruct(a.shape, F32) for a in (lower_block, upper_block, right_side)],
        in_specs=[pl.BlockSpec(memory_space=pl.ANY)] * 3,
        out_specs=[pl.BlockSpec(memory_space=pltpu.VMEM)] * 3,
        scratch_shapes=[
            pltpu.VMEM((LEVELS, 3, rows, order), F32),
            pltpu.VMEM((rows, order), F32),
            pltpu.VMEM((order, order), F32),
            pair(), pair(), pair(), pair(), pair(), pair(),
            one(), one(), one(), one(), one(), one(),
            pair(), pair(),
            pltpu.SemaphoreType.DMA((5,)),
            pltpu.SemaphoreType.DMA((LEVELS, 3, 5)),
            pltpu.SemaphoreType.DMA((LEVELS, 2, 5)),
            pltpu.SemaphoreType.DMA((5,)),
            pltpu.SemaphoreType.DMA((5,)),
            pltpu.VMEM((rows, order), F32),
            pltpu.SemaphoreType.DMA((5,)),
            pltpu.SemaphoreType.DMA((5,)),
        ],
        compiler_params=pltpu.CompilerParams(
            collective_id=0, has_side_effects=True, vmem_limit_bytes=60 * 1024 * 1024
        ),
    )(lower_block, upper_block, right_side)


def solution(mesh):
    placed = (P("layer", None, None), P("layer", None, None), P("layer", None, None))
    return jax.shard_map(
        per_device,
        mesh=mesh,
        in_specs=placed,
        out_specs=placed,
        check_vma=False,
    )
```
